128 devices in a mesh: kring: 8 (over y, x_lo), band: 16 (over z, x_hi, core).
Axes of the slice: x: 4 (x_hi: 2, x_lo: 2; x = x_hi * 2 + x_lo), y: 4, z: 4, core: 2. Of those that a mesh axis runs over, the one named last changes fastest.
Arguments:
- current: bfloat16 [262144, 256], P(('kring', 'band')), may hold values from -61 to 61
- previous: bfloat16 [262144, 256], P(('kring', 'band')), may hold values from -6 to 6
- energies: float32 [262144], P(('kring', 'band')), may hold values from 1.5 to 2.5
- targets: int32 [262144], P(('kring', 'band')), may hold values from 0 to 15, as said below
- layer_ids: int32 [327680], P(('kring', 'band')), may hold values from 0 to 1
- conduction_pairs: bfloat16 [327680, 1024], P(('kring', 'band')), may hold values from -0.375 to 0.375
- valence_pairs: bfloat16 [327680, 1024], P(('kring', 'band')), may hold values from -0.228125 to 0.228125
- exchange_pairs: bfloat16 [327680, 1024], P(('kring', 'band')), may hold values from -0.137001939 to 0.137001939
- screened: bfloat16 [8, 2, 1024, 2, 1024], P(None, None, 'band'), may hold values from -0.03203125 to 1.28203125
- coulomb: float32 [2, 2, 1024], replicated, may hold values from 0.2 to 2
- beta_prev: float32 [256], replicated, may hold values from 0.5 to 2
Outputs:
- next_vector: bfloat16 [262144, 256], P(('kring', 'band'))
- lanczos_alpha: float32 [256], replicated
- lanczos_beta: float32 [256], replicated
The draws below stay inside these ranges and needn't reach their ends.
Inputs may be any that keep to these rules, and one draw needn't show every extreme that they name: `targets`: the 2048 rows of one device name each band index at most 2560 // 16 times; in every k-group one band index is named exactly that often by every device of the group.
All inputs are finite; a program needn't handle non-finite values.
Results may differ from the reference program's by a relative error of at most 0.0057.
Values may be sent and summed in bfloat16 or wider, within the bound.
A program may use at most 128 MiB of HBM per device.

```python
import math
import jax
import jax.numpy as jnp
from jax import lax

NG = 1024
NVEC = 256
OWN_DEV = 2048
SLOT_DEV = 2560
NQ = 8
NTOT = 262144
SLOTS = 327680
N_KRING = 8
N_BAND = 16


def draw_current(key, part):
    row_count = OWN_DEV * N_KRING * N_BAND
    key_a, key_b, key_c = jax.random.split(key, 3)
    values = jnp.clip(jax.random.normal(key_a, (row_count, NVEC), jnp.float32), -4.0, 4.0)
    position = jnp.arange(row_count, dtype=jnp.float32) / row_count
    row_scale = 0.25 * 3.0 ** position * 10.0 ** jax.random.uniform(key_b, (row_count,), jnp.float32)
    column_scale = 2.0 ** jax.random.uniform(key_c, (NVEC,), jnp.float32)
    return (values * row_scale[:, None] * column_scale[None, :]).astype(jnp.bfloat16)


def draw_targets(key, part):
    device_count = N_KRING * N_BAND
    capacity = SLOT_DEV // N_BAND
    key_full, key_rest = jax.random.split(key)
    favored = jax.random.randint(key_full, (N_KRING,), 0, N_BAND).astype(jnp.int32)
    favored_rows = jnp.repeat(favored, N_BAND)

    def one_block(block_key, chosen):
        key_grid, key_perm, key_rows = jax.random.split(block_key, 3)
        grid_ids = jax.random.permutation(key_grid, (N_BAND - 1) * capacity)[:OWN_DEV - capacity].astype(jnp.int32)
        relabel = jax.random.permutation(key_perm, N_BAND - 1).astype(jnp.int32)
        others = jnp.mod(chosen + 1 + relabel[grid_ids // capacity], N_BAND).astype(jnp.int32)
        ordered = jnp.concatenate([jnp.full((capacity,), chosen, jnp.int32), others])
        return ordered[jax.random.permutation(key_rows, OWN_DEV)]
    block_keys = jax.random.split(key_rest, device_count)
    return jax.vmap(one_block)(block_keys, favored_rows).reshape(-1).astype(jnp.int32)


def rough_values(key, shape):
    return jnp.clip(jax.random.normal(key, shape, jnp.float32), -4.0, 4.0)


def band_pairing(key):
    group_keys = jax.random.split(key, N_KRING)

    def one_group(group_key):
        return jax.random.permutation(group_key, N_BAND).astype(jnp.int32)
    return jax.vmap(one_group)(group_keys).reshape(-1).astype(jnp.int32)


def spike_rows(key, row_count):
    pairing = band_pairing(key)
    device_of_row = (jnp.arange(row_count, dtype=jnp.int32) // SLOT_DEV).astype(jnp.int32)
    share_of_row = pairing[device_of_row]
    share_of_column = (jnp.arange(NG, dtype=jnp.int32) // (NG // N_BAND)).astype(jnp.int32)
    return jnp.where(share_of_row[:, None] == share_of_column[None, :], 4.0, 1.0).astype(jnp.float32)


def pair_fields(key):
    row_count = SLOT_DEV * N_KRING * N_BAND
    key_raw, key_noise, key_spike = jax.random.split(jax.random.fold_in(key, 11), 3)
    base_scale = 0.45 * NG ** (-0.5)
    valence = base_scale * rough_values(key_raw, (row_count, NG)) * spike_rows(key_spike, row_count)
    conduction = 1.5 * valence + 0.5 * base_scale * rough_values(key_noise, (row_count, NG))
    return (valence, conduction)


def draw_valence_pairs(key, part):
    return pair_fields(key)[0].astype(jnp.bfloat16)


def draw_conduction_pairs(key, part):
    return pair_fields(key)[1].astype(jnp.bfloat16)


def draw_exchange_pairs(key, part):
    row_count = SLOT_DEV * N_KRING * N_BAND
    key_raw, key_spike, key_sign, key_wave = jax.random.split(jax.random.fold_in(key, 23), 4)
    row_scale = (NG * N_KRING) ** (-0.5)
    random_part = 0.75 * row_scale * rough_values(key_raw, (row_count, NG)) * spike_rows(key_spike, row_count)
    slot_sign = (2 * jax.random.randint(key_sign, (row_count,), 0, 2) - 1).astype(jnp.float32)
    wave_sign = (2 * jax.random.randint(key_wave, (NG,), 0, 2) - 1).astype(jnp.float32)
    return (random_part + 0.2 * row_scale * slot_sign[:, None] * wave_sign[None, :]).astype(jnp.bfloat16)


def draw_screened(key, part):
    key_raw, key_diag = jax.random.split(jax.random.fold_in(key, 37))
    spread = (2 * NG * NQ) ** (-0.5)
    random_part = spread * rough_values(key_raw, (NQ, 2, NG, 2, NG))
    strength = jnp.exp(jax.random.uniform(key_diag, (2, NG), jnp.float32, -1.2039728, 0.18232156))
    first = (jnp.arange(NQ, dtype=jnp.int32) == 0)[:, None, None, None, None]
    layer_index = jnp.arange(2, dtype=jnp.int32)
    same_layer = (layer_index[:, None] == layer_index[None, :])[None, :, None, :, None]
    wave_index = jnp.arange(NG, dtype=jnp.int32)
    same_wave = (wave_index[:, None] == wave_index[None, :])[None, None, :, None, :]
    on_diagonal = first & same_layer & same_wave
    return (random_part + jnp.where(on_diagonal, strength[None, :, :, None, None], 0.0)).astype(jnp.bfloat16)


def with_ends(array, stream_key, low, largest):
    spot = [jax.random.randint(jax.random.fold_in(stream_key, axis), (), 0, length) for axis, length in enumerate(array.shape)]
    main_axis = array.shape.index(max(array.shape))
    neighbour = spot[:main_axis] + [(spot[main_axis] + 1) % array.shape[main_axis]] + spot[main_axis + 1:]
    return array.at[tuple(spot)].set(low).at[tuple(neighbour)].set(largest)


def block_scale(stream_key, dims, pieces, least, high):
    gain = 1.0
    for dim, blocks in pieces:
        heights = jax.random.uniform(jax.random.fold_in(jax.random.fold_in(stream_key, 6), dim), (blocks,), jnp.float32, least / len(pieces), high / len(pieces))
        gain = gain * jnp.repeat(jnp.exp(heights), dims[dim] // blocks).reshape((-1,) + (1,) * (len(dims) - 1 - dim))
    return gain


def centred(own_key, shape, width, reach, pieces=(), kind=jnp.bfloat16):
    array = jax.random.normal(own_key, shape, jnp.float32) * width
    if len(pieces) > 0:
        array = block_scale(own_key, shape, pieces, -0.22, 0.18) * array
    return jnp.clip(array, min=-reach, max=reach).astype(kind)


def setup_inputs(seed: int = 0) -> dict:
    keys = jax.random.split(jax.random.key(seed), 12)
    current = draw_current(jax.random.fold_in(keys[11], 71), 0)
    previous = centred(keys[1], (NTOT, NVEC), 1.0, 6.0, ((0, 128),))
    energies = jnp.clip(1.5 + 1.0 * jax.random.uniform(keys[2], (NTOT,), jnp.float32) ** block_scale(keys[2], (NTOT,), ((0, 128),), -0.2, 0.2), 1.5, 2.5)
    targets = draw_targets(jax.random.fold_in(keys[11], 71), 0)
    layer_ids = with_ends(jax.random.randint(keys[4], (SLOTS,), 0, 2), jax.random.fold_in(keys[4], 1), 0, 1).astype(jnp.int32)
    conduction_pairs = draw_conduction_pairs(jax.random.fold_in(keys[11], 71), 0)
    valence_pairs = draw_valence_pairs(jax.random.fold_in(keys[11], 71), 0)
    exchange_pairs = draw_exchange_pairs(jax.random.fold_in(keys[11], 71), 0)
    screened = draw_screened(jax.random.fold_in(keys[11], 71), 0)
    coulomb = jnp.clip(jnp.exp(jax.random.uniform(keys[9], (2, 2, NG), jnp.float32, math.log(0.2), math.log(2.0))), 0.2, 2.0)
    beta_prev = jnp.clip(jnp.exp(jax.random.uniform(keys[10], (NVEC,), jnp.float32, math.log(0.5), math.log(2.0))), 0.5, 2.0)
    return dict(current=current, previous=previous, energies=energies, targets=targets, layer_ids=layer_ids, conduction_pairs=conduction_pairs, valence_pairs=valence_pairs, exchange_pairs=exchange_pairs, screened=screened, coulomb=coulomb, beta_prev=beta_prev)


epsilon_mean = 1e-06

def place_rows(targets, capacity, band_count):
    onehot = (targets[..., None] == jnp.arange(band_count, dtype=jnp.int32)).astype(jnp.int32)
    counted = jnp.cumsum(onehot, axis=-2)
    ranking = lax.optimization_barrier(jnp.sum(counted * onehot, axis=-1)) - 1
    return ranking

def reference(current, previous, energies, targets, layer_ids, conduction_pairs, valence_pairs, exchange_pairs, screened, coulomb, beta_prev):
    capacity = SLOT_DEV // N_BAND
    owners = targets.reshape(N_KRING, N_BAND, OWN_DEV)
    ranking = place_rows(owners, capacity, N_BAND)
    group_ids = jnp.arange(N_KRING, dtype=jnp.int32)[:, None, None]
    sender = jnp.arange(N_BAND, dtype=jnp.int32)[None, :, None]
    global_slot = ((group_ids * N_BAND + owners) * SLOT_DEV + sender * capacity + ranking).reshape(-1).astype(jnp.int32)
    arrived = jnp.zeros((SLOTS, NVEC), jnp.bfloat16).at[global_slot].set(current)
    layer_pick = (layer_ids[:, None] == jnp.arange(2, dtype=jnp.int32)[None, :]).astype(jnp.bfloat16)
    group_rows = N_BAND * SLOT_DEV
    projected_list = []
    exchange_total = jnp.zeros((2, NG, NVEC), jnp.float32)
    for group_index in range(N_KRING):
        row_start = group_index * group_rows
        split_amps = (arrived[row_start:row_start + group_rows][:, None, :] * layer_pick[row_start:row_start + group_rows][:, :, None]).astype(jnp.float32)
        valence_sum = jnp.einsum('tg,tln->lgn', valence_pairs[row_start:row_start + group_rows].astype(jnp.float32), split_amps)
        projected_list.append(valence_sum.astype(jnp.bfloat16))
        exchange_total = exchange_total + jnp.einsum('tg,tln->lgn', exchange_pairs[row_start:row_start + group_rows].astype(jnp.float32), split_amps)
    coupled = (coulomb[:, 0, :, None] * exchange_total[0][None] + coulomb[:, 1, :, None] * exchange_total[1][None]).astype(jnp.bfloat16)
    coupled_wide = coupled.astype(jnp.float32)
    kernel_list = []
    for group_index in range(N_KRING):
        direct_sum = jnp.zeros((2, NG, NVEC), jnp.float32)
        for source_group in range(N_KRING):
            distance = (group_index - source_group) % NQ
            direct_sum = direct_sum + jnp.einsum('aphg,apn->hgn', screened[distance].astype(jnp.float32), projected_list[source_group].astype(jnp.float32))
        direct = direct_sum.astype(jnp.bfloat16).astype(jnp.float32)
        row_start = group_index * group_rows
        cond_rows = conduction_pairs[row_start:row_start + group_rows].astype(jnp.float32)
        exch_rows = exchange_pairs[row_start:row_start + group_rows].astype(jnp.float32)
        both_direct = jnp.einsum('tg,lgn->tln', cond_rows, direct)
        both_exchange = jnp.einsum('tg,lgn->tln', exch_rows, coupled_wide)
        kernel_all = 2.0 * both_exchange - both_direct
        choose = layer_pick[row_start:row_start + group_rows].astype(jnp.float32)
        kernel_list.append(lax.optimization_barrier(jnp.sum(kernel_all * choose[:, :, None], axis=1)).astype(jnp.bfloat16))
    kernel_rows = jnp.concatenate(kernel_list, axis=0)
    kernel_own = kernel_rows[global_slot].astype(jnp.float32)
    current_wide = current.astype(jnp.float32)
    applied = energies[:, None] * current_wide + kernel_own
    start_vec = applied - beta_prev[None, :] * previous.astype(jnp.float32)
    lanczos_alpha = lax.optimization_barrier(jnp.sum(current_wide * start_vec, axis=0)) / lax.optimization_barrier(jnp.sum(current_wide * current_wide, axis=0))
    residual = start_vec - lanczos_alpha[None, :] * current_wide
    lanczos_beta = jnp.sqrt(lax.optimization_barrier(jnp.sum(residual * residual, axis=0)) / NTOT + epsilon_mean)
    next_vector = (residual / lanczos_beta[None, :]).astype(jnp.bfloat16)
    return (next_vector, lanczos_alpha, lanczos_beta)
```

```python
import functools

import jax
import jax.numpy as jnp
from jax import lax
from jax.experimental import pallas as pl
from jax.experimental.pallas import tpu as pltpu
from jax.sharding import PartitionSpec as P

MESH = pl.DeviceIdType.MESH
F32 = jnp.float32
BF16 = jnp.bfloat16
epsilon_mean = 1e-06


def dot(a, b):
    return jnp.dot(a, b, preferred_element_type=F32)


def loop(low, high, body):
    def step(index, carry):
        body(index)
        return carry

    lax.fori_loop(low, high, step, 0)


def aligned(index, size):
    return pl.ds(pl.multiple_of(index * size, size), size)


def kernel(
    dims,
    targets_ref,
    layers_ref,
    energies_ref,
    coulomb_ref,
    beta_prev_ref,
    current_hbm,
    previous_hbm,
    conduction_hbm,
    valence_hbm,
    exchange_hbm,
    screened_hbm,
    next_ref,
    alpha_ref,
    beta_ref,
    current,
    previous,
    conduction,
    valence,
    exchange,
    screened,
    outgoing,
    arrived,
    amps_t,
    gather_mat,
    slot_row,
    slot_col,
    layer_col,
    energy_col,
    part_v,
    part_e,
    pair_buf,
    chip_sum,
    reduced_in,
    low_send,
    proj_mine,
    proj_all,
    total_part,
    total_in,
    coupled_part,
    coupled_t,
    tile_out,
    coupled_all,
    direct_all,
    exchange_rows,
    kernel_out,
    returned,
    start,
    stats_mine,
    stats_in,
    stats_group,
    stats_all,
    hbm_sem,
    first_send,
    first_recv,
    pair_send,
    pair_recv,
    scatter_send,
    scatter_recv,
    half_send,
    half_recv,
    ring_send,
    ring_recv,
    gather_send,
    gather_recv,
    forward_send,
    forward_recv,
    last_send,
    last_recv,
    stat_send,
    stat_recv,
    stat_ring_send,
    stat_ring_recv,
):
    KR, B, NZ, CAP, OWN, SLOT, NG, NV = dims
    NB = B // 2
    NX = NB // NZ
    W = B // NZ
    GC = NG // NB
    GD = NG // B
    NH = NV // 2
    NK = NH // KR
    CH = SLOT // NZ
    LANE = min(128, NH)
    rows_total = OWN * KR * B

    g = lax.axis_index("kring")
    s = lax.axis_index("band")
    chip = s // 2
    core = lax.rem(s, 2)
    other = 1 - core
    plane = chip // NX
    column = lax.rem(chip, NX)
    partner = chip * 2 + other

    def chip_at(jc):
        return lax.rem(plane + jc // NX, NZ) * NX + lax.rem(column + lax.rem(jc, NX), NX)

    def chip_from(jc):
        return lax.rem(plane + NZ - jc // NX, NZ) * NX + lax.rem(column + NX - lax.rem(jc, NX), NX)

    def band_at(j):
        return chip_at(j // 2) * 2 + lax.rem(core + lax.rem(j, 2), 2)

    def band_from(j):
        return chip_from(j // 2) * 2 + lax.rem(core + lax.rem(j, 2), 2)

    def ring_at(k):
        return lax.rem(g + k, KR)

    def ring_from(k):
        return lax.rem(g + KR - k, KR)

    def remote(src, dst, send, recv, ring, band):
        return pltpu.make_async_remote_copy(
            src_ref=src,
            dst_ref=dst,
            send_sem=send,
            recv_sem=recv,
            device_id=(ring, band),
            device_id_type=MESH,
        )

    fetches = [
        pltpu.make_async_copy(src, dst, hbm_sem.at[i])
        for i, (src, dst) in enumerate(
            (
                (current_hbm, current),
                (valence_hbm, valence),
                (exchange_hbm, exchange),
                (previous_hbm, previous),
                (screened_hbm, screened),
                (conduction_hbm, conduction),
            )
        )
    ]
    for fetch in fetches:
        fetch.start()

    barrier = pltpu.get_barrier_semaphore()

    def greet_band(j):
        pl.semaphore_signal(barrier, inc=1, device_id=(g, band_at(j)), device_id_type=MESH)

    def greet_ring(k):
        pl.semaphore_signal(barrier, inc=1, device_id=(ring_at(k), s), device_id_type=MESH)

    loop(1, B, greet_band)
    loop(1, KR, greet_ring)

    blk = min(256, OWN)
    upper = (
        lax.broadcasted_iota(jnp.int32, (blk, blk), 0) <= lax.broadcasted_iota(jnp.int32, (blk, blk), 1)
    ).astype(F32).astype(BF16)
    carry = jnp.zeros((B, 1), F32)
    for b in range(OWN // blk):
        targets = targets_ref[:, b * blk : (b + 1) * blk]
        onehot = (lax.broadcasted_iota(jnp.int32, (B, blk), 0) == targets).astype(F32)
        counted = dot(onehot.astype(BF16), upper) + carry
        rank = jnp.sum(counted * onehot, axis=0, keepdims=True) - 1.0
        slot_row[:, b * blk : (b + 1) * blk] = targets.astype(F32) * CAP + rank
        carry = carry + jnp.sum(onehot, axis=1, keepdims=True)

    pl.semaphore_wait(barrier, B - 1 + KR - 1)
    fetches[0].wait()

    def first_copy(j):
        return remote(
            outgoing.at[j],
            arrived.at[pl.ds(pl.multiple_of(s * CAP, CAP), CAP), :],
            first_send.at[j],
            first_recv.at[j],
            g,
            band_at(j),
        )

    def place(target):
        wanted = (lax.broadcasted_iota(jnp.int32, (CAP, 1), 0) + target * CAP).astype(F32)
        pick = (wanted == slot_row[...]).astype(F32).astype(BF16)
        return dot(pick, current[...]).astype(BF16)

    def send_first(j):
        outgoing[j] = place(band_at(j))
        first_copy(j).start()

    loop(1, B, send_first)
    arrived[pl.ds(pl.multiple_of(s * CAP, CAP), CAP), :] = place(s)

    def column_of(row_ref, col_ref, count):
        def one(b):
            row = row_ref[:, aligned(b, LANE)].astype(F32)
            col_ref[aligned(b, LANE), :] = jnp.broadcast_to(row, (LANE, LANE)).T

        loop(0, count // LANE, one)

    column_of(slot_row, slot_col, OWN)
    column_of(layers_ref, layer_col, SLOT)
    column_of(energies_ref, energy_col, OWN)

    def build_gather(b):
        wanted = (lax.broadcasted_iota(jnp.int32, (1, LANE), 1) + b * LANE).astype(F32)
        gather_mat[:, aligned(b, LANE)] = (slot_col[...] == wanted).astype(F32).astype(BF16)

    loop(0, SLOT // LANE, build_gather)

    def wide(col, rows):
        return jnp.concatenate([col[rows, :]] * (NV // LANE), axis=1)

    tile = min(256, OWN)
    fetches[3].wait()

    def begin_start(b):
        rows = aligned(b, tile)
        start[rows, :] = wide(energy_col, rows) * current[rows, :].astype(F32) - beta_prev_ref[
            ...
        ] * previous[rows, :].astype(F32)

    loop(0, OWN // tile, begin_start)

    fetches[1].wait()
    fetches[2].wait()

    wide_tile = min(256, NG)

    def project(i):
        rows = aligned(lax.rem(plane + NZ - i, NZ), CH)
        amps = arrived[rows, :].astype(F32).T
        layers = layers_ref[:, rows]
        amps_t[i, 0:NV, :] = jnp.where(layers == 0, amps, 0.0).astype(BF16)
        amps_t[i, NV : 2 * NV, :] = jnp.where(layers == 1, amps, 0.0).astype(BF16)

    def accumulate(i, pairs, part):
        rows = aligned(lax.rem(plane + NZ - i, NZ), CH)

        def one(b):
            cols = aligned(b, wide_tile)
            more = dot(amps_t[i], pairs[rows, cols]).reshape(2, NV, wide_tile)
            if i == 0:
                part[:, :, cols] = more
            else:
                part[:, :, cols] += more

        loop(0, NG // wide_tile, one)

    for i in range(NZ):
        loop(max(1, i * W), (i + 1) * W, lambda j: first_copy(j).wait_recv())
        project(i)
        if i < NZ - 1:
            accumulate(i, valence, part_v)
            accumulate(i, exchange, part_e)

    def pair_copy(which, part):
        return remote(
            part.at[:, pl.ds(pl.multiple_of(other * NH, NH), NH), :],
            pair_buf.at[which],
            pair_send.at[which],
            pair_recv.at[which],
            g,
            partner,
        )

    def scatter_copy(which, jc):
        return remote(
            chip_sum.at[which, chip_at(jc)],
            reduced_in.at[which, jc],
            scatter_send.at[which, jc],
            scatter_recv.at[which, jc],
            g,
            chip_at(jc) * 2 + core,
        )

    def scatter(which, part):
        pair_copy(which, part).wait_recv()

        def one(jc):
            to = chip_at(jc)
            cols = aligned(to, GC)
            chip_sum[which, to] = (
                part[:, pl.ds(pl.multiple_of(core * NH, NH), NH), cols] + pair_buf[which, :, :, cols]
            ).astype(BF16)
            scatter_copy(which, jc).start()

        loop(1, NB, one)

    def reduce(which, part):
        cols = aligned(chip, GC)
        total = part[:, pl.ds(pl.multiple_of(core * NH, NH), NH), cols] + pair_buf[which, :, :, cols]
        for jc in range(1, NB):
            scatter_copy(which, jc).wait_recv()
            total = total + reduced_in[which, jc].astype(F32)
        return total

    accumulate(NZ - 1, valence, part_v)
    pair_copy(0, part_v).start()
    accumulate(NZ - 1, exchange, part_e)
    pair_copy(1, part_e).start()
    scatter(0, part_v)
    scatter(1, part_e)

    total = reduce(0, part_v)
    first_half = lax.broadcasted_iota(jnp.int32, (NH, GC), 1) < GD
    swapped = pltpu.roll(total[1], GD, 1)
    swapped_too = pltpu.roll(total[0], GD, 1)
    for_core = (
        jnp.where(first_half, total[0], swapped).astype(BF16),
        jnp.where(first_half, swapped_too, total[1]).astype(BF16),
    )
    mine = pl.ds(pl.multiple_of(core * NH, NH), NH)

    @pl.when(core == 0)
    def _():
        proj_mine[mine, :] = for_core[0]
        low_send[...] = for_core[1]

    @pl.when(core == 1)
    def _():
        proj_mine[mine, :] = for_core[1]
        low_send[...] = for_core[0]

    half_copy = remote(low_send, proj_mine.at[mine, :], half_send, half_recv, g, partner)
    half_copy.start()

    def ring_copy(k):
        return remote(
            proj_mine,
            proj_all.at[:, k * GC : (k + 1) * GC],
            ring_send.at[0, k],
            ring_recv.at[0, k],
            ring_at(k),
            s,
        )

    def total_copy(k):
        return remote(
            total_part.at[:, pl.ds(pl.multiple_of(ring_at(k) * NK, NK), NK), :],
            total_in.at[k],
            ring_send.at[1, k],
            ring_recv.at[1, k],
            ring_at(k),
            s,
        )

    def coupled_copy(k):
        return remote(
            coupled_part,
            coupled_t.at[:, pl.ds(pl.multiple_of(g * NK, NK), NK), :],
            ring_send.at[2, k],
            ring_recv.at[2, k],
            ring_at(k),
            s,
        )

    half_copy.wait_recv()
    for k in range(1, KR):
        ring_copy(k).start()
    proj_all[:, 0:GC] = proj_mine[...]

    total_part[...] = reduce(1, part_e)
    for k in range(1, KR):
        total_copy(k).start()

    fetches[4].wait()
    for k in range(1, KR):
        ring_copy(k).wait_recv()
    part_x = part_v
    pair_copy(0, part_v).wait_send()

    def direct_tile(b):
        cols = aligned(b, wide_tile)
        for layer in range(2):
            part_x[layer, :, cols] = dot(proj_all[...], screened[layer, :, cols])

    loop(0, NG // wide_tile, direct_tile)
    pair_copy(2, part_x).start()

    ring_total = total_part[:, pl.ds(pl.multiple_of(g * NK, NK), NK), :]
    for k in range(1, KR):
        total_copy(k).wait_recv()
        ring_total = ring_total + total_in[k]
    here = aligned(chip, GC)
    coupled_part[0] = coulomb_ref[0:1, here] * ring_total[0] + coulomb_ref[1:2, here] * ring_total[1]
    coupled_part[1] = coulomb_ref[2:3, here] * ring_total[0] + coulomb_ref[3:4, here] * ring_total[1]
    for k in range(1, KR):
        coupled_copy(k).start()
    coupled_t[:, pl.ds(pl.multiple_of(g * NK, NK), NK), :] = coupled_part[...]

    scatter(2, part_x)

    half_cols = pl.ds(pl.multiple_of(core * NH, NH), NH)

    def gather_copy(which, full, jc):
        return remote(
            tile_out.at[which],
            full.at[:, aligned(chip, GC), half_cols],
            gather_send.at[which, jc],
            gather_recv.at[which, jc],
            g,
            chip_at(jc) * 2 + core,
        )

    def forward_copy(which, full, jc):
        block = full.at[:, aligned(chip_from(jc), GC), half_cols]
        return remote(
            block, block, forward_send.at[which, jc], forward_recv.at[which, jc], g, partner
        )

    def spread(which, full, block_t):
        for layer in range(2):
            tile_out[which, layer] = block_t[layer].T.astype(BF16)
        loop(1, NB, lambda jc: gather_copy(which, full, jc).start())
        full[:, aligned(chip, GC), half_cols] = tile_out[which]
        forward_copy(which, full, 0).start()

    def collect(which, full):
        def one(jc):
            gather_copy(which, full, jc).wait_recv()
            forward_copy(which, full, jc).start()

        loop(1, NB, one)

    for k in range(1, KR):
        coupled_copy(k).wait_recv()
    spread(0, coupled_all, coupled_t[...])
    direct_block = reduce(2, part_x)
    spread(1, direct_all, direct_block)
    collect(0, coupled_all)
    loop(0, NB, lambda jc: forward_copy(0, coupled_all, jc).wait_recv())

    pair_rows = 2 * CAP

    def exchange_tile(b):
        rows = aligned(b, pair_rows)
        zero = dot(exchange[rows, :], coupled_all[0])
        one = dot(exchange[rows, :], coupled_all[1])
        exchange_rows[rows, :] = 2.0 * jnp.where(wide(layer_col, rows) == 0.0, zero, one)

    loop(0, NB, exchange_tile)
    fetches[5].wait()
    collect(1, direct_all)
    loop(0, NB, lambda jc: forward_copy(1, direct_all, jc).wait_recv())

    def last_copy(j):
        to = band_at(j)
        return remote(
            kernel_out.at[pl.ds(pl.multiple_of(to * CAP, CAP), CAP), :],
            returned.at[pl.ds(pl.multiple_of(s * CAP, CAP), CAP), :],
            last_send.at[j],
            last_recv.at[j],
            g,
            to,
        )

    def kernel_tile(jc):
        rows = aligned(chip_at(jc), pair_rows)
        zero = dot(conduction[rows, :], direct_all[0])
        one = dot(conduction[rows, :], direct_all[1])
        direct = jnp.where(wide(layer_col, rows) == 0.0, zero, one)
        kernel_out[rows, :] = (exchange_rows[rows, :] - direct).astype(BF16)

    def kernel_step(jc):
        kernel_tile(jc)
        last_copy(2 * jc).start()
        last_copy(2 * jc + 1).start()

    loop(1, NB, kernel_step)
    kernel_tile(0)
    last_copy(1).start()
    own = pl.ds(pl.multiple_of(s * CAP, CAP), CAP)
    returned[own, :] = kernel_out[own, :]

    for i in range(NZ):
        loop(max(1, i * W), (i + 1) * W, lambda j: last_copy(j).wait_recv())
        slots = aligned(lax.rem(plane + NZ - i, NZ), CH)

        def add_rows(b, slots=slots):
            rows = aligned(b, tile)
            start[rows, :] += dot(gather_mat[rows, slots], returned[slots, :])

        loop(0, OWN // tile, add_rows)

    def fold(b, sums):
        rows = aligned(b, tile)
        cur = current[rows, :].astype(F32)
        return (
            sums[0] + jnp.sum(cur * start[rows, :], axis=0, keepdims=True),
            sums[1] + jnp.sum(cur * cur, axis=0, keepdims=True),
        )

    none = jnp.zeros((1, NV), F32)
    cross, square = lax.fori_loop(0, OWN // tile, fold, (none, none))

    def ratio(above, below):
        return above / jnp.where(below == 0.0, 1.0, below)

    local = ratio(cross, square)

    def fold_rest(b, acc):
        rows = aligned(b, tile)
        rest = start[rows, :] - local * current[rows, :].astype(F32)
        return acc + jnp.sum(rest * rest, axis=0, keepdims=True)

    rest_sq = lax.fori_loop(0, OWN // tile, fold_rest, none)

    def combine(read, count):
        cross = sum(read(i)[0:1] for i in range(count))
        square = sum(read(i)[1:2] for i in range(count))
        alpha = ratio(cross, square)
        rest = none
        for i in range(count):
            item = read(i)
            apart = ratio(item[0:1], item[1:2]) - alpha
            rest = rest + (item[2:3] + apart * apart * item[1:2])
        return cross, square, rest

    stats_mine[...] = jnp.concatenate([cross, square, rest_sq] + [none] * 5, axis=0)

    def stat_copy(j):
        return remote(stats_mine, stats_in.at[s], stat_send.at[j], stat_recv.at[j], g, band_at(j))

    def stat_ring_copy(k):
        return remote(
            stats_group, stats_all.at[g], stat_ring_send.at[k], stat_ring_recv.at[k], ring_at(k), s
        )

    loop(1, B, lambda j: stat_copy(j).start())
    stats_in[s] = stats_mine[...]
    loop(1, B, lambda j: stat_copy(j).wait_recv())
    stats_group[...] = jnp.concatenate(
        list(combine(lambda i: stats_in[i], B)) + [none] * 5, axis=0
    )
    loop(1, KR, lambda k: stat_ring_copy(k).start())
    stats_all[g] = stats_group[...]
    loop(1, KR, lambda k: stat_ring_copy(k).wait_recv())
    cross, square, rest_sq = combine(lambda i: stats_all[i], KR)

    alpha = cross / square
    beta = jnp.sqrt(rest_sq / rows_total + epsilon_mean)
    alpha_ref[...] = alpha
    beta_ref[...] = beta

    def finish(b):
        rows = aligned(b, tile)
        next_ref[rows, :] = (
            (start[rows, :] - alpha * current[rows, :].astype(F32)) / beta
        ).astype(BF16)

    loop(0, OWN // tile, finish)

    loop(1, B, lambda j: first_copy(j).wait_send())
    pair_copy(1, part_e).wait_send()
    pair_copy(2, part_x).wait_send()
    half_copy.wait_send()
    for which in range(3):
        loop(1, NB, lambda jc, which=which: scatter_copy(which, jc).wait_send())
    for k in range(1, KR):
        ring_copy(k).wait_send()
        total_copy(k).wait_send()
        coupled_copy(k).wait_send()
    for which, full in ((0, coupled_all), (1, direct_all)):
        loop(1, NB, lambda jc, which=which, full=full: gather_copy(which, full, jc).wait_send())
        loop(0, NB, lambda jc, which=which, full=full: forward_copy(which, full, jc).wait_send())
    loop(1, B, lambda j: last_copy(j).wait_send())
    loop(1, B, lambda j: stat_copy(j).wait_send())
    loop(1, KR, lambda k: stat_ring_copy(k).wait_send())


def per_device(
    planes,
    current,
    previous,
    energies,
    targets,
    layer_ids,
    conduction_pairs,
    valence_pairs,
    exchange_pairs,
    screened,
    coulomb,
    beta_prev,
):
    KR, B = lax.axis_size("kring"), lax.axis_size("band")
    OWN, NV = current.shape
    SLOT, NG = conduction_pairs.shape
    CAP = SLOT // B
    NB = B // 2
    NH = NV // 2
    GC = NG // NB
    GD = NG // B
    NK = NH // KR
    CH = SLOT // planes
    LANE = min(128, NH)
    by_layer = jnp.transpose(screened, (3, 0, 1, 2, 4)).reshape(2, KR * 2 * GD, NG)
    vmem = pltpu.VMEM
    dma = pltpu.SemaphoreType.DMA
    scratch = [
        vmem((OWN, NV), BF16),
        vmem((OWN, NV), BF16),
        vmem((SLOT, NG), BF16),
        vmem((SLOT, NG), BF16),
        vmem((SLOT, NG), BF16),
        vmem((2, KR * 2 * GD, NG), BF16),
        vmem((B, CAP, NV), BF16),
        vmem((SLOT, NV), BF16),
        vmem((planes, 2 * NV, CH), BF16),
        vmem((OWN, SLOT), BF16),
        vmem((1, OWN), F32),
        vmem((OWN, LANE), F32),
        vmem((SLOT, LANE), F32),
        vmem((OWN, LANE), F32),
        vmem((2, NV, NG), F32),
        vmem((2, NV, NG), F32),
        vmem((3, 2, NH, NG), F32),
        vmem((3, NB, 2, NH, GC), BF16),
        vmem((3, NB, 2, NH, GC), BF16),
        vmem((NH, GC), BF16),
        vmem((NV, GC), BF16),
        vmem((NV, KR * GC), BF16),
        vmem((2, NH, GC), F32),
        vmem((KR, 2, NK, GC), F32),
        vmem((2, NK, GC), F32),
        vmem((2, NH, GC), F32),
        vmem((2, 2, GC, NH), BF16),
        vmem((2, NG, NV), BF16),
        vmem((2, NG, NV), BF16),
        vmem((SLOT, NV), F32),
        vmem((SLOT, NV), BF16),
        vmem((SLOT, NV), BF16),
        vmem((OWN, NV), F32),
        vmem((8, NV), F32),
        vmem((B, 8, NV), F32),
        vmem((8, NV), F32),
        vmem((KR, 8, NV), F32),
        dma((6,)),
        dma((B,)),
        dma((B,)),
        dma((3,)),
        dma((3,)),
        dma((3, NB)),
        dma((3, NB)),
        dma,
        dma,
        dma((3, KR)),
        dma((3, KR)),
        dma((2, NB)),
        dma((2, NB)),
        dma((2, NB)),
        dma((2, NB)),
        dma((B,)),
        dma((B,)),
        dma((B,)),
        dma((B,)),
        dma((KR,)),
        dma((KR,)),
    ]
    in_vmem = pl.BlockSpec(memory_space=pltpu.VMEM)
    in_hbm = pl.BlockSpec(memory_space=pl.ANY)
    next_vector, alpha, beta = pl.pallas_call(
        functools.partial(kernel, (KR, B, planes, CAP, OWN, SLOT, NG, NV)),
        out_shape=(
            jax.ShapeDtypeStruct((OWN, NV), BF16),
            jax.ShapeDtypeStruct((1, NV), F32),
            jax.ShapeDtypeStruct((1, NV), F32),
        ),
        in_specs=[in_vmem] * 5 + [in_hbm] * 6,
        out_specs=(in_vmem, in_vmem, in_vmem),
        scratch_shapes=scratch,
        compiler_params=pltpu.CompilerParams(
            collective_id=0, has_side_effects=True, vmem_limit_bytes=62 * 1024 * 1024
        ),
    )(
        targets.reshape(1, OWN),
        layer_ids.reshape(1, SLOT),
        energies.reshape(1, OWN),
        coulomb.reshape(4, NG),
        beta_prev.reshape(1, NV),
        current,
        previous,
        conduction_pairs,
        valence_pairs,
        exchange_pairs,
        by_layer,
    )
    return next_vector, alpha.reshape(NV), beta.reshape(NV)


def solution(mesh):
    in_specs = (
        P(("kring", "band"), None),
        P(("kring", "band"), None),
        P(("kring", "band")),
        P(("kring", "band")),
        P(("kring", "band")),
        P(("kring", "band"), None),
        P(("kring", "band"), None),
        P(("kring", "band"), None),
        P(None, None, "band", None, None),
        P(),
        P(),
    )
    out_specs = (P(("kring", "band"), None), P(), P())
    planes = max(2, mesh.shape["band"] // 4)
    return jax.shard_map(
        functools.partial(per_device, planes),
        mesh=mesh,
        in_specs=in_specs,
        out_specs=out_specs,
        check_vma=False,
    )
```

```python
import functools

import jax
import jax.numpy as jnp
from jax import lax
from jax.experimental import pallas as pl
from jax.experimental.pallas import tpu as pltpu
from jax.sharding import PartitionSpec as P

MESH = pl.DeviceIdType.MESH
F32 = jnp.float32
BF16 = jnp.bfloat16
epsilon_mean = 1e-06


def dot(a, b):
    return jnp.dot(a, b, preferred_element_type=F32)


def loop(low, high, body):
    def step(index, carry):
        body(index)
        return carry

    lax.fori_loop(low, high, step, 0)


def aligned(index, size):
    return pl.ds(pl.multiple_of(index * size, size), size)


def kernel(
    dims,
    targets_ref,
    layers_ref,
    energies_ref,
    coulomb_ref,
    beta_prev_ref,
    current_hbm,
    previous_hbm,
    conduction_hbm,
    valence_hbm,
    exchange_hbm,
    raw_hbm,
    start,
    lanczos,
    current,
    previous,
    valence,
    exchange,
    raw,
    screened,
    outgoing,
    arrived,
    amps_t,
    gather_mat,
    slot_row,
    layer_row,
    slot_col,
    layer_col,
    energy_col,
    part_v,
    part_e,
    pair_buf,
    chip_sum,
    reduced_in,
    chip_sum_e,
    reduced_e,
    proj_mine,
    proj_all,
    part_x,
    total_part,
    total_in,
    coupled_part,
    coupled_t,
    coupled_tile,
    direct_tile,
    coupled_all,
    direct_all,
    exchange_rows,
    kernel_out,
    returned,
    stats_mine,
    stats_in,
    stats_group,
    stats_all,
    hbm_sem,
    raw_sem,
    first_send,
    first_recv,
    pair_send,
    pair_recv,
    scatter_send,
    scatter_recv,
    share_send,
    share_recv,
    ring_send,
    ring_recv,
    y_send,
    y_recv,
    layer_send,
    layer_recv,
    coupled_send,
    coupled_recv,
    gather_send,
    gather_recv,
    forward_send,
    forward_recv,
    last_send,
    last_recv,
    stat_send,
    stat_recv,
    stat_ring_send,
    stat_ring_recv,
):
    KR, B, NZ, CAP, OWN, SLOT, NG, NV = dims
    NB = B // 2
    NX = NB // NZ
    W = B // NZ
    GC = NG // NB
    GD = NG // B
    NH = NV // 2
    CH = SLOT // NZ
    LANE = min(128, NH)
    rows_total = OWN * KR * B
    conduction = valence

    g = lax.axis_index("kring")
    s = lax.axis_index("band")
    chip = s // 2
    core = lax.rem(s, 2)
    other = 1 - core
    plane = chip // NX
    column = lax.rem(chip, NX)
    partner = chip * 2 + other

    planes_at = [lax.rem(plane + i, NZ) for i in range(NZ)]
    columns_at = [lax.rem(column + i, NX) for i in range(NX)]
    rings_at = [lax.rem(g + k, KR) for k in range(KR)]
    cores_at = (core, other)
    chips_at = [planes_at[jc // NX] * NX + columns_at[jc % NX] for jc in range(NB)]
    chips_from = [planes_at[-(jc // NX) % NZ] * NX + columns_at[-(jc % NX) % NX] for jc in range(NB)]
    peers_at = [chips_at[j // 2] * 2 + cores_at[j % 2] for j in range(B)]

    phases = (
        sorted({1, NZ - 1}),
        [i for i in range(NZ) if i not in (1, NZ - 1)][::-1],
    )
    plane_order = phases[0] + phases[1]
    away = [i * NX + t for i in plane_order for t in reversed(range(NX)) if i + t > 0]

    def chips_of(planes):
        return [i * NX + t for i in planes for t in reversed(range(NX))]

    def peers_of(planes):
        return [2 * jc + t for jc in chips_of(planes) for t in (1, 0) if jc + t > 0]

    KY = KR // 2
    GY = NG // KY
    NQ = 2 * NB
    NE = NH // NQ
    ring_y = g // 2
    ring_x = lax.rem(g, 2)
    ys_at = [lax.rem(ring_y + t, KY) for t in range(KY)]
    xs_at = (ring_x, 1 - ring_x)
    layer_at = [(xs_at[q // NB], chips_at[q % NB]) for q in range(NQ)]
    layer_here = ring_x * NB + chip

    def remote(src, dst, send, recv, ring, band):
        return pltpu.make_async_remote_copy(
            src_ref=src,
            dst_ref=dst,
            send_sem=send,
            recv_sem=recv,
            device_id=(ring, band),
            device_id_type=MESH,
        )

    waits = []
    later = waits.append

    def drain():
        for wait in waits:
            wait()

    fetches = [
        pltpu.make_async_copy(src, dst, hbm_sem.at[i])
        for i, (src, dst) in enumerate(
            (
                (current_hbm, current),
                (valence_hbm, valence),
                (exchange_hbm, exchange),
                (previous_hbm, previous),
                (conduction_hbm, conduction),
            )
        )
    ]
    fetches[0].start()

    barrier = pltpu.get_barrier_semaphore()
    for j in range(1, B):
        pl.semaphore_signal(barrier, inc=1, device_id=(g, peers_at[j]), device_id_type=MESH)
    for k in range(1, KR):
        pl.semaphore_signal(barrier, inc=1, device_id=(rings_at[k], s), device_id_type=MESH)
    for x, c in layer_at[NB + 1 :]:
        pl.semaphore_signal(
            barrier, inc=1, device_id=(ring_y * 2 + x, c * 2 + core), device_id_type=MESH
        )

    blk = min(256, OWN)
    upper = (
        lax.broadcasted_iota(jnp.int32, (blk, blk), 0) <= lax.broadcasted_iota(jnp.int32, (blk, blk), 1)
    ).astype(F32).astype(BF16)
    carry = jnp.zeros((B, 1), F32)
    for b in range(OWN // blk):
        targets = targets_ref[:, b * blk : (b + 1) * blk]
        onehot = (lax.broadcasted_iota(jnp.int32, (B, blk), 0) == targets).astype(F32)
        counted = dot(onehot.astype(BF16), upper) + carry
        rank = jnp.sum(counted * onehot, axis=0, keepdims=True) - 1.0
        slot_row[:, b * blk : (b + 1) * blk] = targets.astype(F32) * CAP + rank
        carry = carry + jnp.sum(onehot, axis=1, keepdims=True)

    fetches[0].wait()

    def raw_fetch(ka):
        slot = lax.rem(ka, 2)
        return pltpu.make_async_copy(raw_hbm.at[ka], raw.at[slot], raw_sem.at[slot])

    raw_fetch(0).start()
    for fetch in fetches[1:4]:
        fetch.start()

    def first_copy(j):
        return remote(
            outgoing.at[j],
            arrived.at[aligned(s, CAP), :],
            first_send.at[j],
            first_recv.at[j],
            g,
            peers_at[j],
        )

    def place(target):
        wanted = (lax.broadcasted_iota(jnp.int32, (CAP, 1), 0) + target * CAP).astype(F32)
        pick = (wanted == slot_row[...]).astype(F32).astype(BF16)
        return dot(pick, current[...]).astype(BF16)

    for j in range(1, B):
        outgoing[j] = place(peers_at[j])
    arrived[aligned(s, CAP), :] = place(s)
    pl.semaphore_wait(barrier, B - 1 + KR - 1 + NB - 1)
    for j in peers_of(phases[0]):
        first_copy(j).start()

    def column_of(row_ref, col_ref, count):
        def one(b):
            row = row_ref[:, aligned(b, LANE)].astype(F32)
            col_ref[aligned(b, LANE), :] = jnp.broadcast_to(row, (LANE, LANE)).T

        loop(0, count // LANE, one)

    for b in range(SLOT // LANE):
        row = layers_ref[b : b + 1, :].astype(F32)
        layer_row[:, b * LANE : (b + 1) * LANE] = row
        layer_col[b * LANE : (b + 1) * LANE, :] = jnp.broadcast_to(row, (LANE, LANE)).T
    GL = min(128, NG)
    JH = 2 * (NG // GL)
    PB = min(GD, 256 // JH)
    place_to = lax.broadcasted_iota(jnp.int32, (JH * PB, JH * PB), 0)
    place_from = lax.broadcasted_iota(jnp.int32, (JH * PB, JH * PB), 1)
    part_layers = (
        (place_to - (place_to // PB) * PB) * JH + place_to // PB == place_from
    ).astype(F32).astype(BF16)

    def part(ka):
        raw_fetch(ka).wait()

        @pl.when(ka + 1 < 2 * KR)
        def _():
            raw_fetch(ka + 1).start()

        slot = lax.rem(ka, 2)
        for b in range(GD // PB):
            rows = dot(part_layers, raw[slot, b * PB * JH : (b + 1) * PB * JH, :]).astype(BF16)
            for jh in range(JH):
                screened[jh % 2, ka, core, b * PB : (b + 1) * PB, jh // 2 * GL : (jh // 2 + 1) * GL] = (
                    rows[jh * PB : (jh + 1) * PB]
                )

    loop(0, 2 * KR, part)
    for j in peers_of(phases[0]):
        first_copy(j).wait_send()
    for j in peers_of(phases[1]):
        first_copy(j).start()
        later(first_copy(j).wait_send)
    shared = screened.at[:, :, core]
    share = remote(shared, shared, share_send, share_recv, g, partner)
    share.start()
    later(share.wait_send)

    def build_gather():
        column_of(slot_row, slot_col, OWN)

        def one(b):
            wanted = (lax.broadcasted_iota(jnp.int32, (1, LANE), 1) + b * LANE).astype(F32)
            gather_mat[:, aligned(b, LANE)] = (slot_col[...] == wanted).astype(F32).astype(BF16)

        loop(0, SLOT // LANE, one)

    def wide(col, rows):
        return jnp.concatenate([col[rows, :]] * (NV // LANE), axis=1)

    tile = min(256, OWN)

    def build_start():
        column_of(energies_ref, energy_col, OWN)

        def one(b):
            rows = aligned(b, tile)
            start[rows, :] = wide(energy_col, rows) * current[rows, :].astype(F32) - beta_prev_ref[
                ...
            ] * previous[rows, :].astype(F32)

        loop(0, OWN // tile, one)

    for fetch in fetches[1:4]:
        fetch.wait()

    plane_cols = NX * GC

    def source_rows(i):
        return aligned(planes_at[-i % NZ], CH)

    def project(i):
        amps = arrived[source_rows(i), :].astype(F32).T
        layers = layer_row[:, source_rows(i)]
        amps_t[i, 0:NV, :] = jnp.where(layers == 0.0, amps, 0.0).astype(BF16)
        amps_t[i, NV : 2 * NV, :] = jnp.where(layers == 1.0, amps, 0.0).astype(BF16)

    def accumulate(phase, pairs, part, cols):
        more = sum(dot(amps_t[i], pairs[source_rows(i), cols]) for i in phases[phase])
        more = more.reshape(2, NV, plane_cols)
        if phase == 0:
            part[:, :, cols] = more
        else:
            part[:, :, cols] += more

    for phase in range(2):
        for j in peers_of(phases[phase]):
            first_copy(j).wait_recv()
        for i in phases[phase]:
            project(i)
        if phase == 0:
            for pairs, part in ((valence, part_v), (exchange, part_e)):
                loop(
                    0,
                    NZ,
                    lambda b, pairs=pairs, part=part: accumulate(
                        0, pairs, part, aligned(b, plane_cols)
                    ),
                )

    mine = aligned(core, NH)
    here = aligned(chip, GC)

    def pair_copy(which, part, i):
        cols = aligned(planes_at[i], plane_cols)
        return remote(
            part.at[:, aligned(other, NH), cols],
            pair_buf.at[which, :, :, cols],
            pair_send.at[which, i],
            pair_recv.at[which, i],
            g,
            partner,
        )

    def pair_sum(which, part, i):
        cols = aligned(planes_at[i], plane_cols)
        accumulate(1, (valence, exchange)[which], part, cols)
        pair_copy(which, part, i).start()
        later(pair_copy(which, part, i).wait_send)

    def scatter_copy(which, jc):
        return remote(
            chip_sum.at[which, jc],
            reduced_in.at[which, jc],
            scatter_send.at[which, jc],
            scatter_recv.at[which, jc],
            g,
            chips_at[jc] * 2 + core,
        )

    def chip_part(which, part, jc):
        cols = aligned(chips_at[jc], GC)
        return part[:, mine, cols] + pair_buf[which, :, :, cols]

    def direct_part(which, part, jc):
        return part[:, :, aligned(chips_at[jc], GC)]

    def send_part(which, jc, value):
        chip_sum[which, jc] = value.astype(BF16)
        scatter_copy(which, jc).start()
        later(scatter_copy(which, jc).wait_send)

    def scatter(which, part):
        for i in plane_order:
            pair_copy(which, part, i).wait_recv()
            for jc in range((i + 1) * NX - 1, max(i * NX - 1, 0), -1):
                send_part(which, jc, chip_part(which, part, jc))

    def reduce(which, part, read):
        total = read(which, part, 0)
        for jc in away:
            scatter_copy(which, jc).wait_recv()
            total = total + reduced_in[which, jc].astype(F32)
        return total

    for i in plane_order:
        pair_sum(0, part_v, i)
    for i in plane_order:
        pair_sum(1, part_e, i)
    scatter(0, part_v)

    def over_y(t):
        return remote(
            chip_sum_e.at[t],
            reduced_e.at[t],
            y_send.at[0, t],
            y_recv.at[0, t],
            ys_at[t] * 2 + ring_x,
            s,
        )

    def exchange_part(t):
        cols = aligned(ys_at[t], GY)
        return part_e[:, mine, cols] + pair_buf[1, :, :, cols]

    for i in plane_order:
        pair_copy(1, part_e, i).wait_recv()
    y_order = sorted(range(1, KY), key=lambda t: -min(t, KY - t))
    for t in y_order:
        chip_sum_e[t] = exchange_part(t).astype(BF16)
        over_y(t).start()
        later(over_y(t).wait_send)

    total = reduce(0, part_v, chip_part)
    for layer in range(2):
        proj_mine[:, layer * GC : (layer + 1) * GC] = total[layer].astype(BF16)

    def ring_copy(k):
        return remote(
            proj_mine,
            proj_all.at[:, 2 * k * GC : 2 * (k + 1) * GC],
            ring_send.at[k],
            ring_recv.at[k],
            rings_at[k],
            s,
        )

    for k in range(1, KR):
        ring_copy(k).start()
        later(ring_copy(k).wait_send)
    proj_all[:, 0 : 2 * GC] = proj_mine[...]

    total_e = exchange_part(0)
    for t in y_order:
        over_y(t).wait_recv()
        total_e = total_e + reduced_e[t].astype(F32)
    total_part[...] = total_e

    def over_layer(q):
        x, c = layer_at[q]
        return remote(
            total_part.at[:, aligned(x * NB + c, NE), :],
            total_in.at[q],
            layer_send.at[0, q],
            layer_recv.at[0, q],
            ring_y * 2 + x,
            c * 2 + core,
        )

    def coupled_copy(q):
        x, c = layer_at[q]
        return remote(
            coupled_part,
            coupled_t.at[:, aligned(layer_here, NE), :],
            layer_send.at[1, q],
            layer_recv.at[1, q],
            ring_y * 2 + x,
            c * 2 + core,
        )

    for q in range(1, NQ):
        over_layer(q).start()
        later(over_layer(q).wait_send)
    build_gather()
    layer_total = total_part[:, aligned(layer_here, NE), :]
    for q in range(1, NQ):
        over_layer(q).wait_recv()
        layer_total = layer_total + total_in[q]
    quarter = aligned(ring_y, GY)
    for layer in range(2):
        coupled_part[layer] = (
            coulomb_ref[layer, 0:1, quarter] * layer_total[0]
            + coulomb_ref[layer, 1:2, quarter] * layer_total[1]
        )
    for q in range(1, NQ):
        coupled_copy(q).start()
        later(coupled_copy(q).wait_send)
    coupled_t[:, aligned(layer_here, NE), :] = coupled_part[...]

    fetches[4].start()
    share.wait_recv()
    for k in range(1, KR):
        ring_copy(k).wait_recv()
    for i in plane_order:
        cols = aligned(planes_at[i], plane_cols)
        for layer in range(2):
            part_x[layer, :, cols] = dot(
                proj_all[...], screened[layer, :, :, :, cols].reshape(2 * KR * GC, plane_cols)
            )
        for jc in range((i + 1) * NX - 1, max(i * NX - 1, 0), -1):
            send_part(1, jc, direct_part(1, part_x, jc))

    def y_copy(t):
        return remote(
            coupled_tile,
            coupled_all.at[:, quarter, mine],
            y_send.at[1, t],
            y_recv.at[1, t],
            ys_at[t] * 2 + ring_x,
            s,
        )

    def coupled_forward(t):
        block = coupled_all.at[:, aligned(ys_at[-t % KY], GY), mine]
        return remote(
            block, block, coupled_send.at[t], coupled_recv.at[t], g, partner
        )

    for q in range(1, NQ):
        coupled_copy(q).wait_recv()
    for layer in range(2):
        coupled_tile[layer] = coupled_t[layer].T.astype(BF16)
    for t in y_order:
        y_copy(t).start()
        later(y_copy(t).wait_send)
    coupled_all[:, quarter, mine] = coupled_tile[...]
    coupled_forward(0).start()
    later(coupled_forward(0).wait_send)
    build_start()

    def gather_copy(jc):
        return remote(
            direct_tile,
            direct_all.at[:, here, mine],
            gather_send.at[jc],
            gather_recv.at[jc],
            g,
            chips_at[jc] * 2 + core,
        )

    def forward_copy(jc):
        block = direct_all.at[:, aligned(chips_from[jc], GC), mine]
        return remote(block, block, forward_send.at[jc], forward_recv.at[jc], g, partner)

    direct_block = reduce(1, part_x, direct_part)
    for layer in range(2):
        direct_tile[layer] = direct_block[layer].T.astype(BF16)
    for jc in away:
        gather_copy(jc).start()
        later(gather_copy(jc).wait_send)
    direct_all[:, here, mine] = direct_tile[...]
    forward_copy(0).start()
    later(forward_copy(0).wait_send)
    for t in y_order:
        y_copy(t).wait_recv()
        coupled_forward(t).start()
        later(coupled_forward(t).wait_send)
    for t in range(KY):
        coupled_forward(t).wait_recv()

    pair_rows = 2 * CAP

    def exchange_tile(b):
        rows = aligned(b, pair_rows)
        zero = dot(exchange[rows, :], coupled_all[0])
        one = dot(exchange[rows, :], coupled_all[1])
        exchange_rows[rows, :] = 2.0 * jnp.where(wide(layer_col, rows) == 0.0, zero, one)

    loop(0, NB, exchange_tile)
    fetches[4].wait()
    for jc in away:
        gather_copy(jc).wait_recv()
        forward_copy(jc).start()
        later(forward_copy(jc).wait_send)
    for jc in range(NB):
        forward_copy(jc).wait_recv()

    def last_copy(j):
        return remote(
            kernel_out.at[aligned(peers_at[j], CAP), :],
            returned.at[aligned(s, CAP), :],
            last_send.at[j],
            last_recv.at[j],
            g,
            peers_at[j],
        )

    def kernel_tile(jc):
        rows = aligned(chips_at[jc], pair_rows)
        zero = dot(conduction[rows, :], direct_all[0])
        one = dot(conduction[rows, :], direct_all[1])
        direct = jnp.where(wide(layer_col, rows) == 0.0, zero, one)
        kernel_out[rows, :] = (exchange_rows[rows, :] - direct).astype(BF16)

    for jc in chips_of(phases[0]):
        kernel_tile(jc)
        for j in (2 * jc + 1, 2 * jc):
            last_copy(j).start()
    for jc in chips_of(phases[1]):
        kernel_tile(jc)
    for j in peers_of(phases[0]):
        last_copy(j).wait_send()
    for j in peers_of(phases[1]):
        last_copy(j).start()
        later(last_copy(j).wait_send)
    own = aligned(s, CAP)
    returned[own, :] = kernel_out[own, :]

    for phase in range(2):
        for j in peers_of(phases[phase]):
            last_copy(j).wait_recv()

        def add_rows(b, phase=phase):
            rows = aligned(b, tile)
            start[rows, :] += sum(
                dot(gather_mat[rows, source_rows(i)], returned[source_rows(i), :])
                for i in phases[phase]
            )

        loop(0, OWN // tile, add_rows)

    def fold(b, sums):
        rows = aligned(b, tile)
        cur = current[rows, :].astype(F32)
        return (
            sums[0] + jnp.sum(cur * start[rows, :], axis=0, keepdims=True),
            sums[1] + jnp.sum(cur * cur, axis=0, keepdims=True),
        )

    none = jnp.zeros((1, NV), F32)
    cross, square = lax.fori_loop(0, OWN // tile, fold, (none, none))

    def ratio(above, below):
        return above / jnp.where(below == 0.0, 1.0, below)

    local = ratio(cross, square)

    def fold_rest(b, acc):
        rows = aligned(b, tile)
        rest = start[rows, :] - local * current[rows, :].astype(F32)
        return acc + jnp.sum(rest * rest, axis=0, keepdims=True)

    rest_sq = lax.fori_loop(0, OWN // tile, fold_rest, none)

    def combine(read, count):
        cross = sum(read(i)[0:1] for i in range(count))
        square = sum(read(i)[1:2] for i in range(count))
        alpha = ratio(cross, square)
        rest = none
        for i in range(count):
            item = read(i)
            apart = ratio(item[0:1], item[1:2]) - alpha
            rest = rest + (item[2:3] + apart * apart * item[1:2])
        return cross, square, rest

    stats_mine[...] = jnp.concatenate([cross, square, rest_sq] + [none] * 5, axis=0)

    def stat_copy(j):
        return remote(
            stats_mine, stats_in.at[s], stat_send.at[j], stat_recv.at[j], g, peers_at[j]
        )

    def stat_ring_copy(k):
        return remote(
            stats_group,
            stats_all.at[g],
            stat_ring_send.at[k],
            stat_ring_recv.at[k],
            rings_at[k],
            s,
        )

    for j in range(1, B):
        stat_copy(j).start()
        later(stat_copy(j).wait_send)
    stats_in[s] = stats_mine[...]
    for j in range(1, B):
        stat_copy(j).wait_recv()
    stats_group[...] = jnp.concatenate(
        list(combine(lambda i: stats_in[i], B)) + [none] * 5, axis=0
    )
    for k in range(1, KR):
        stat_ring_copy(k).start()
        later(stat_ring_copy(k).wait_send)
    stats_all[g] = stats_group[...]
    for k in range(1, KR):
        stat_ring_copy(k).wait_recv()
    cross, square, rest_sq = combine(lambda i: stats_all[i], KR)

    alpha = cross / square
    beta = jnp.sqrt(rest_sq / rows_total + epsilon_mean)
    lanczos[...] = jnp.concatenate([alpha, beta] + [none] * 6, axis=0)

    drain()


def finish(start_ref, current_ref, lanczos_ref, next_ref, alpha_ref, beta_ref):
    alpha = lanczos_ref[0:1, :]
    beta = lanczos_ref[1:2, :]
    next_ref[...] = ((start_ref[...] - alpha * current_ref[...].astype(F32)) / beta).astype(BF16)
    alpha_ref[...] = alpha
    beta_ref[...] = beta


def per_device(
    planes,
    current,
    previous,
    energies,
    targets,
    layer_ids,
    conduction_pairs,
    valence_pairs,
    exchange_pairs,
    screened,
    coulomb,
    beta_prev,
):
    KR, B = lax.axis_size("kring"), lax.axis_size("band")
    OWN, NV = current.shape
    SLOT, NG = conduction_pairs.shape
    CAP = SLOT // B
    NB = B // 2
    NH = NV // 2
    GC = NG // NB
    GD = NG // B
    CH = SLOT // planes
    KY = KR // 2
    GY = NG // KY
    NQ = B
    NE = NH // NQ
    LANE = min(128, NH)
    GL = min(128, NG)
    J = NG // GL
    by_rows = jnp.transpose(screened.reshape(KR, 2, GD, 2, J, GL), (0, 1, 2, 4, 3, 5)).reshape(
        2 * KR, GD * J * 2, GL
    )
    vmem = pltpu.VMEM
    dma = pltpu.SemaphoreType.DMA
    scratch = [
        vmem((OWN, NV), BF16),
        vmem((OWN, NV), BF16),
        vmem((SLOT, NG), BF16),
        vmem((SLOT, NG), BF16),
        vmem((2, GD * J * 2, GL), BF16),
        vmem((2, KR * 2, 2, GD, NG), BF16),
        vmem((B, CAP, NV), BF16),
        vmem((SLOT, NV), BF16),
        vmem((planes, 2 * NV, CH), BF16),
        vmem((OWN, SLOT), BF16),
        vmem((1, OWN), F32),
        vmem((1, SLOT), F32),
        vmem((OWN, LANE), F32),
        vmem((SLOT, LANE), F32),
        vmem((OWN, LANE), F32),
        vmem((2, NV, NG), F32),
        vmem((2, NV, NG), F32),
        vmem((2, 2, NH, NG), F32),
        vmem((2, NB, 2, NH, GC), BF16),
        vmem((2, NB, 2, NH, GC), BF16),
        vmem((KY, 2, NH, GY), BF16),
        vmem((KY, 2, NH, GY), BF16),
        vmem((NH, 2 * GC), BF16),
        vmem((NH, KR * 2 * GC), BF16),
        vmem((2, NH, NG), F32),
        vmem((2, NH, GY), F32),
        vmem((NQ, 2, NE, GY), F32),
        vmem((2, NE, GY), F32),
        vmem((2, NH, GY), F32),
        vmem((2, GY, NH), BF16),
        vmem((2, GC, NH), BF16),
        vmem((2, NG, NV), BF16),
        vmem((2, NG, NV), BF16),
        vmem((SLOT, NV), F32),
        vmem((SLOT, NV), BF16),
        vmem((SLOT, NV), BF16),
        vmem((8, NV), F32),
        vmem((B, 8, NV), F32),
        vmem((8, NV), F32),
        vmem((KR, 8, NV), F32),
        dma((5,)),
        dma((2,)),
        dma((B,)),
        dma((B,)),
        dma((2, planes)),
        dma((2, planes)),
        dma((2, NB)),
        dma((2, NB)),
        dma,
        dma,
        dma((KR,)),
        dma((KR,)),
        dma((2, KY)),
        dma((2, KY)),
        dma((2, NQ)),
        dma((2, NQ)),
        dma((KY,)),
        dma((KY,)),
        dma((NB,)),
        dma((NB,)),
        dma((NB,)),
        dma((NB,)),
        dma((B,)),
        dma((B,)),
        dma((B,)),
        dma((B,)),
        dma((KR,)),
        dma((KR,)),
    ]
    in_vmem = pl.BlockSpec(memory_space=pltpu.VMEM)
    in_hbm = pl.BlockSpec(memory_space=pl.ANY)
    start, lanczos = pl.pallas_call(
        functools.partial(kernel, (KR, B, planes, CAP, OWN, SLOT, NG, NV)),
        out_shape=(
            jax.ShapeDtypeStruct((OWN, NV), F32),
            jax.ShapeDtypeStruct((8, NV), F32),
        ),
        in_specs=[in_vmem] * 5 + [in_hbm] * 6,
        out_specs=(in_vmem, in_vmem),
        scratch_shapes=scratch,
        compiler_params=pltpu.CompilerParams(
            collective_id=0, has_side_effects=True, vmem_limit_bytes=62 * 1024 * 1024
        ),
    )(
        targets.reshape(1, OWN),
        layer_ids.reshape(SLOT // LANE, LANE),
        energies.reshape(1, OWN),
        coulomb,
        beta_prev.reshape(1, NV),
        current,
        previous,
        conduction_pairs,
        valence_pairs,
        exchange_pairs,
        by_rows,
    )
    rows = OWN // 4
    next_vector, alpha, beta = pl.pallas_call(
        finish,
        grid=(4,),
        out_shape=(
            jax.ShapeDtypeStruct((OWN, NV), BF16),
            jax.ShapeDtypeStruct((1, NV), F32),
            jax.ShapeDtypeStruct((1, NV), F32),
        ),
        in_specs=[
            pl.BlockSpec((rows, NV), lambda b: (b, 0)),
            pl.BlockSpec((rows, NV), lambda b: (b, 0)),
            pl.BlockSpec((8, NV), lambda b: (0, 0)),
        ],
        out_specs=(
            pl.BlockSpec((rows, NV), lambda b: (b, 0)),
            pl.BlockSpec((1, NV), lambda b: (0, 0)),
            pl.BlockSpec((1, NV), lambda b: (0, 0)),
        ),
    )(start, current, lanczos)
    return next_vector, alpha.reshape(NV), beta.reshape(NV)


def solution(mesh):
    in_specs = (
        P(("kring", "band"), None),
        P(("kring", "band"), None),
        P(("kring", "band")),
        P(("kring", "band")),
        P(("kring", "band")),
        P(("kring", "band"), None),
        P(("kring", "band"), None),
        P(("kring", "band"), None),
        P(None, None, "band", None, None),
        P(),
        P(),
    )
    out_specs = (P(("kring", "band"), None), P(), P())
    planes = max(2, mesh.shape["band"] // 4)
    return jax.shard_map(
        functools.partial(per_device, planes),
        mesh=mesh,
        in_specs=in_specs,
        out_specs=out_specs,
        check_vma=False,
    )
```

```python
import functools

import jax
import jax.numpy as jnp
from jax import lax
from jax.experimental import pallas as pl
from jax.experimental.pallas import tpu as pltpu
from jax.sharding import PartitionSpec as P

MESH = pl.DeviceIdType.MESH
F32 = jnp.float32
BF16 = jnp.bfloat16
epsilon_mean = 1e-06


def dot(a, b):
    return jnp.dot(a, b, preferred_element_type=F32)


def loop(low, high, body):
    def step(index, carry):
        body(index)
        return carry

    lax.fori_loop(low, high, step, 0)


def aligned(index, size):
    return pl.ds(pl.multiple_of(index * size, size), size)


def kernel(
    dims,
    targets_ref,
    layers_ref,
    energies_ref,
    coulomb_ref,
    beta_prev_ref,
    current_hbm,
    previous_hbm,
    conduction_hbm,
    valence_hbm,
    exchange_hbm,
    raw_hbm,
    start,
    lanczos,
    current,
    previous,
    valence,
    exchange,
    raw,
    screened,
    outgoing,
    arrived,
    amps_t,
    gather_mat,
    slot_row,
    layer_row,
    slot_col,
    layer_col,
    energy_col,
    part_v,
    part_e,
    pair_buf,
    chip_sum,
    reduced_in,
    chip_sum_e,
    reduced_e,
    proj_mine,
    proj_all,
    part_x,
    total_part,
    total_in,
    coupled_part,
    coupled_t,
    coupled_tile,
    direct_tile,
    coupled_all,
    direct_all,
    exchange_rows,
    kernel_out,
    returned,
    stats_mine,
    stats_in,
    stats_group,
    stats_all,
    hbm_sem,
    raw_sem,
    first_send,
    first_recv,
    pair_send,
    pair_recv,
    scatter_send,
    scatter_recv,
    share_send,
    share_recv,
    ring_send,
    ring_recv,
    y_send,
    y_recv,
    layer_send,
    layer_recv,
    coupled_send,
    coupled_recv,
    gather_send,
    gather_recv,
    forward_send,
    forward_recv,
    last_send,
    last_recv,
    stat_send,
    stat_recv,
    stat_ring_send,
    stat_ring_recv,
):
    KR, B, NZ, CAP, OWN, SLOT, NG, NV = dims
    NB = B // 2
    NX = NB // NZ
    W = B // NZ
    GC = NG // NB
    GD = NG // B
    NH = NV // 2
    CH = SLOT // NZ
    LANE = min(128, NH)
    rows_total = OWN * KR * B
    conduction = valence

    g = lax.axis_index("kring")
    s = lax.axis_index("band")
    chip = s // 2
    core = lax.rem(s, 2)
    other = 1 - core
    plane = chip // NX
    column = lax.rem(chip, NX)
    partner = chip * 2 + other

    planes_at = [lax.rem(plane + i, NZ) for i in range(NZ)]
    columns_at = [lax.rem(column + i, NX) for i in range(NX)]
    rings_at = [lax.rem(g + k, KR) for k in range(KR)]
    cores_at = (core, other)
    chips_at = [planes_at[jc // NX] * NX + columns_at[jc % NX] for jc in range(NB)]
    chips_from = [planes_at[-(jc // NX) % NZ] * NX + columns_at[-(jc % NX) % NX] for jc in range(NB)]
    peers_at = [chips_at[j // 2] * 2 + cores_at[j % 2] for j in range(B)]

    phases = (
        sorted({1, NZ - 1}),
        [i for i in range(NZ) if i not in (1, NZ - 1)][::-1],
    )
    plane_order = phases[0] + phases[1]
    away = [i * NX + t for i in plane_order for t in reversed(range(NX)) if i + t > 0]

    def chips_of(planes):
        return [i * NX + t for i in planes for t in reversed(range(NX))]

    def peers_of(planes):
        return [2 * jc + t for jc in chips_of(planes) for t in (1, 0) if jc + t > 0]

    KY = KR // 2
    GY = NG // KY
    NQ = 2 * NB
    NE = NH // NQ
    ring_y = g // 2
    ring_x = lax.rem(g, 2)
    ys_at = [lax.rem(ring_y + t, KY) for t in range(KY)]
    xs_at = (ring_x, 1 - ring_x)
    layer_at = [(xs_at[q // NB], chips_at[q % NB]) for q in range(NQ)]
    layer_here = ring_x * NB + chip

    def remote(src, dst, send, recv, ring, band):
        return pltpu.make_async_remote_copy(
            src_ref=src,
            dst_ref=dst,
            send_sem=send,
            recv_sem=recv,
            device_id=(ring, band),
            device_id_type=MESH,
        )

    waits = []
    later = waits.append

    def drain():
        for wait in waits:
            wait()

    fetches = [
        pltpu.make_async_copy(src, dst, hbm_sem.at[i])
        for i, (src, dst) in enumerate(
            (
                (current_hbm, current),
                (valence_hbm, valence),
                (exchange_hbm, exchange),
                (previous_hbm, previous),
                (conduction_hbm, conduction),
            )
        )
    ]
    fetches[0].start()

    barrier = pltpu.get_barrier_semaphore()
    for j in range(1, B):
        pl.semaphore_signal(barrier, inc=1, device_id=(g, peers_at[j]), device_id_type=MESH)
    for k in range(1, KR):
        pl.semaphore_signal(barrier, inc=1, device_id=(rings_at[k], s), device_id_type=MESH)
    for x, c in layer_at[NB + 1 :]:
        pl.semaphore_signal(
            barrier, inc=1, device_id=(ring_y * 2 + x, c * 2 + core), device_id_type=MESH
        )

    blk = min(256, OWN)
    upper = (
        lax.broadcasted_iota(jnp.int32, (blk, blk), 0) <= lax.broadcasted_iota(jnp.int32, (blk, blk), 1)
    ).astype(F32).astype(BF16)
    carry = jnp.zeros((B, 1), F32)
    for b in range(OWN // blk):
        targets = targets_ref[:, b * blk : (b + 1) * blk]
        onehot = (lax.broadcasted_iota(jnp.int32, (B, blk), 0) == targets).astype(F32)
        counted = dot(onehot.astype(BF16), upper) + carry
        rank = jnp.sum(counted * onehot, axis=0, keepdims=True) - 1.0
        slot_row[:, b * blk : (b + 1) * blk] = targets.astype(F32) * CAP + rank
        carry = carry + jnp.sum(onehot, axis=1, keepdims=True)

    fetches[0].wait()

    def raw_fetch(ka):
        slot = lax.rem(ka, 2)
        return pltpu.make_async_copy(raw_hbm.at[ka], raw.at[slot], raw_sem.at[slot])

    raw_fetch(0).start()
    for fetch in fetches[1:4]:
        fetch.start()

    def first_copy(j):
        return remote(
            outgoing.at[j],
            arrived.at[aligned(s, CAP), :],
            first_send.at[j],
            first_recv.at[j],
            g,
            peers_at[j],
        )

    def place(target):
        wanted = (lax.broadcasted_iota(jnp.int32, (CAP, 1), 0) + target * CAP).astype(F32)
        pick = (wanted == slot_row[...]).astype(F32).astype(BF16)
        return dot(pick, current[...]).astype(BF16)

    for j in range(1, B):
        outgoing[j] = place(peers_at[j])
    arrived[aligned(s, CAP), :] = place(s)
    pl.semaphore_wait(barrier, B - 1 + KR - 1 + NB - 1)
    for j in peers_of(phases[0]):
        first_copy(j).start()

    def column_of(row_ref, col_ref, count):
        def one(b):
            row = row_ref[:, aligned(b, LANE)].astype(F32)
            col_ref[aligned(b, LANE), :] = jnp.broadcast_to(row, (LANE, LANE)).T

        loop(0, count // LANE, one)

    for b in range(SLOT // LANE):
        row = layers_ref[b : b + 1, :].astype(F32)
        layer_row[:, b * LANE : (b + 1) * LANE] = row
        layer_col[b * LANE : (b + 1) * LANE, :] = jnp.broadcast_to(row, (LANE, LANE)).T
    GL = min(128, NG)
    JH = 2 * (NG // GL)
    PB = min(GD, 256 // JH)
    place_to = lax.broadcasted_iota(jnp.int32, (JH * PB, JH * PB), 0)
    place_from = lax.broadcasted_iota(jnp.int32, (JH * PB, JH * PB), 1)
    part_layers = (
        (place_to - (place_to // PB) * PB) * JH + place_to // PB == place_from
    ).astype(F32).astype(BF16)

    def part(ka):
        raw_fetch(ka).wait()

        @pl.when(ka + 1 < 2 * KR)
        def _():
            raw_fetch(ka + 1).start()

        slot = lax.rem(ka, 2)
        for b in range(GD // PB):
            rows = dot(part_layers, raw[slot, b * PB * JH : (b + 1) * PB * JH, :]).astype(BF16)
            for jh in range(JH):
                screened[jh % 2, ka, core, b * PB : (b + 1) * PB, jh // 2 * GL : (jh // 2 + 1) * GL] = (
                    rows[jh * PB : (jh + 1) * PB]
                )

    first_part = KR + KR // 4
    loop(0, first_part, part)
    for j in peers_of(phases[0]):
        first_copy(j).wait_send()
    for j in peers_of(phases[1]):
        first_copy(j).start()
        later(first_copy(j).wait_send)
    loop(first_part, 2 * KR, part)
    shared = screened.at[:, :, core]
    share = remote(shared, shared, share_send, share_recv, g, partner)
    share.start()
    later(share.wait_send)

    def build_gather():
        column_of(slot_row, slot_col, OWN)

        def one(b):
            wanted = (lax.broadcasted_iota(jnp.int32, (1, LANE), 1) + b * LANE).astype(F32)
            gather_mat[:, aligned(b, LANE)] = (slot_col[...] == wanted).astype(F32).astype(BF16)

        loop(0, SLOT // LANE, one)

    def wide(col, rows):
        return jnp.concatenate([col[rows, :]] * (NV // LANE), axis=1)

    tile = min(256, OWN)

    def build_start():
        column_of(energies_ref, energy_col, OWN)

        def one(b):
            rows = aligned(b, tile)
            start[rows, :] = wide(energy_col, rows) * current[rows, :].astype(F32) - beta_prev_ref[
                ...
            ] * previous[rows, :].astype(F32)

        loop(0, OWN // tile, one)

    for fetch in fetches[1:4]:
        fetch.wait()

    plane_cols = NX * GC

    def source_rows(i):
        return aligned(planes_at[-i % NZ], CH)

    def project(i):
        amps = arrived[source_rows(i), :].astype(F32).T
        layers = layer_row[:, source_rows(i)]
        amps_t[i, 0:NV, :] = jnp.where(layers == 0.0, amps, 0.0).astype(BF16)
        amps_t[i, NV : 2 * NV, :] = jnp.where(layers == 1.0, amps, 0.0).astype(BF16)

    def accumulate(phase, pairs, part, cols):
        more = sum(dot(amps_t[i], pairs[source_rows(i), cols]) for i in phases[phase])
        more = more.reshape(2, NV, plane_cols)
        if phase == 0:
            part[:, :, cols] = more
        else:
            part[:, :, cols] += more

    for phase in range(2):
        for j in peers_of(phases[phase]):
            first_copy(j).wait_recv()
        for i in phases[phase]:
            project(i)
        if phase == 0:
            for pairs, part in ((valence, part_v), (exchange, part_e)):
                loop(
                    0,
                    NZ,
                    lambda b, pairs=pairs, part=part: accumulate(
                        0, pairs, part, aligned(b, plane_cols)
                    ),
                )

    mine = aligned(core, NH)
    here = aligned(chip, GC)

    def pair_copy(which, part, i):
        cols = aligned(planes_at[i], plane_cols)
        return remote(
            part.at[:, aligned(other, NH), cols],
            pair_buf.at[which, :, :, cols],
            pair_send.at[which, i],
            pair_recv.at[which, i],
            g,
            partner,
        )

    def pair_sum(which, part, i):
        cols = aligned(planes_at[i], plane_cols)
        accumulate(1, (valence, exchange)[which], part, cols)
        pair_copy(which, part, i).start()
        later(pair_copy(which, part, i).wait_send)

    def scatter_copy(which, jc):
        return remote(
            chip_sum.at[which, jc],
            reduced_in.at[which, jc],
            scatter_send.at[which, jc],
            scatter_recv.at[which, jc],
            g,
            chips_at[jc] * 2 + core,
        )

    def chip_part(which, part, jc):
        cols = aligned(chips_at[jc], GC)
        return part[:, mine, cols] + pair_buf[which, :, :, cols]

    def direct_part(which, part, jc):
        return part[:, :, aligned(chips_at[jc], GC)]

    def send_part(which, jc, value):
        chip_sum[which, jc] = value.astype(BF16)
        scatter_copy(which, jc).start()
        later(scatter_copy(which, jc).wait_send)

    def scatter(which, part):
        for i in plane_order:
            pair_copy(which, part, i).wait_recv()
            for jc in range((i + 1) * NX - 1, max(i * NX - 1, 0), -1):
                send_part(which, jc, chip_part(which, part, jc))

    def reduce(which, part, read):
        total = read(which, part, 0)
        for jc in away:
            scatter_copy(which, jc).wait_recv()
            total = total + reduced_in[which, jc].astype(F32)
        return total

    for i in plane_order:
        pair_sum(0, part_v, i)
    for i in plane_order:
        pair_sum(1, part_e, i)
    scatter(0, part_v)

    def over_y(t):
        return remote(
            chip_sum_e.at[t],
            reduced_e.at[t],
            y_send.at[0, t],
            y_recv.at[0, t],
            ys_at[t] * 2 + ring_x,
            s,
        )

    def exchange_part(t):
        cols = aligned(ys_at[t], GY)
        return part_e[:, mine, cols] + pair_buf[1, :, :, cols]

    for i in plane_order:
        pair_copy(1, part_e, i).wait_recv()
    y_order = sorted(range(1, KY), key=lambda t: -min(t, KY - t))
    for t in y_order:
        chip_sum_e[t] = exchange_part(t).astype(BF16)
        over_y(t).start()
        later(over_y(t).wait_send)

    total = reduce(0, part_v, chip_part)
    for layer in range(2):
        proj_mine[:, layer * GC : (layer + 1) * GC] = total[layer].astype(BF16)

    def ring_copy(k):
        return remote(
            proj_mine,
            proj_all.at[:, 2 * k * GC : 2 * (k + 1) * GC],
            ring_send.at[k],
            ring_recv.at[k],
            rings_at[k],
            s,
        )

    for k in range(1, KR):
        ring_copy(k).start()
        later(ring_copy(k).wait_send)
    proj_all[:, 0 : 2 * GC] = proj_mine[...]

    total_e = exchange_part(0)
    for t in y_order:
        over_y(t).wait_recv()
        total_e = total_e + reduced_e[t].astype(F32)
    total_part[...] = total_e

    def over_layer(q):
        x, c = layer_at[q]
        return remote(
            total_part.at[:, aligned(x * NB + c, NE), :],
            total_in.at[q],
            layer_send.at[0, q],
            layer_recv.at[0, q],
            ring_y * 2 + x,
            c * 2 + core,
        )

    def coupled_copy(q):
        x, c = layer_at[q]
        return remote(
            coupled_part,
            coupled_t.at[:, aligned(layer_here, NE), :],
            layer_send.at[1, q],
            layer_recv.at[1, q],
            ring_y * 2 + x,
            c * 2 + core,
        )

    for q in range(1, NQ):
        over_layer(q).start()
        later(over_layer(q).wait_send)
    fetches[4].start()
    share.wait_recv()
    for k in range(1, KR):
        ring_copy(k).wait_recv()
    for i in plane_order:
        cols = aligned(planes_at[i], plane_cols)
        for layer in range(2):
            part_x[layer, :, cols] = dot(
                proj_all[...], screened[layer, :, :, :, cols].reshape(2 * KR * GC, plane_cols)
            )
        for jc in range((i + 1) * NX - 1, max(i * NX - 1, 0), -1):
            send_part(1, jc, direct_part(1, part_x, jc))

    layer_total = total_part[:, aligned(layer_here, NE), :]
    for q in range(1, NQ):
        over_layer(q).wait_recv()
        layer_total = layer_total + total_in[q]
    quarter = aligned(ring_y, GY)
    for layer in range(2):
        coupled_part[layer] = (
            coulomb_ref[layer, 0:1, quarter] * layer_total[0]
            + coulomb_ref[layer, 1:2, quarter] * layer_total[1]
        )
    for q in range(1, NQ):
        coupled_copy(q).start()
        later(coupled_copy(q).wait_send)
    coupled_t[:, aligned(layer_here, NE), :] = coupled_part[...]

    def y_copy(t):
        return remote(
            coupled_tile,
            coupled_all.at[:, quarter, mine],
            y_send.at[1, t],
            y_recv.at[1, t],
            ys_at[t] * 2 + ring_x,
            s,
        )

    def coupled_forward(t):
        block = coupled_all.at[:, aligned(ys_at[-t % KY], GY), mine]
        return remote(
            block, block, coupled_send.at[t], coupled_recv.at[t], g, partner
        )

    for q in range(1, NQ):
        coupled_copy(q).wait_recv()
    for layer in range(2):
        coupled_tile[layer] = coupled_t[layer].T.astype(BF16)
    for t in y_order:
        y_copy(t).start()
        later(y_copy(t).wait_send)
    coupled_all[:, quarter, mine] = coupled_tile[...]
    coupled_forward(0).start()
    later(coupled_forward(0).wait_send)

    def gather_copy(jc):
        return remote(
            direct_tile,
            direct_all.at[:, here, mine],
            gather_send.at[jc],
            gather_recv.at[jc],
            g,
            chips_at[jc] * 2 + core,
        )

    def forward_copy(jc):
        block = direct_all.at[:, aligned(chips_from[jc], GC), mine]
        return remote(block, block, forward_send.at[jc], forward_recv.at[jc], g, partner)

    direct_block = reduce(1, part_x, direct_part)
    for layer in range(2):
        direct_tile[layer] = direct_block[layer].T.astype(BF16)
    for jc in away:
        gather_copy(jc).start()
        later(gather_copy(jc).wait_send)
    direct_all[:, here, mine] = direct_tile[...]
    forward_copy(0).start()
    later(forward_copy(0).wait_send)
    for t in y_order:
        y_copy(t).wait_recv()
        coupled_forward(t).start()
        later(coupled_forward(t).wait_send)
    for t in range(KY):
        coupled_forward(t).wait_recv()

    pair_rows = 2 * CAP

    def exchange_tile(b):
        rows = aligned(b, pair_rows)
        zero = dot(exchange[rows, :], coupled_all[0])
        one = dot(exchange[rows, :], coupled_all[1])
        exchange_rows[rows, :] = 2.0 * jnp.where(wide(layer_col, rows) == 0.0, zero, one)

    loop(0, NB, exchange_tile)
    fetches[4].wait()
    for jc in away:
        gather_copy(jc).wait_recv()
        forward_copy(jc).start()
        later(forward_copy(jc).wait_send)
    for jc in range(NB):
        forward_copy(jc).wait_recv()

    def last_copy(j):
        return remote(
            kernel_out.at[aligned(peers_at[j], CAP), :],
            returned.at[aligned(s, CAP), :],
            last_send.at[j],
            last_recv.at[j],
            g,
            peers_at[j],
        )

    def kernel_tile(jc):
        rows = aligned(chips_at[jc], pair_rows)
        zero = dot(conduction[rows, :], direct_all[0])
        one = dot(conduction[rows, :], direct_all[1])
        direct = jnp.where(wide(layer_col, rows) == 0.0, zero, one)
        kernel_out[rows, :] = (exchange_rows[rows, :] - direct).astype(BF16)

    for jc in chips_of(phases[0]):
        kernel_tile(jc)
        for j in (2 * jc + 1, 2 * jc):
            last_copy(j).start()
    for jc in chips_of(phases[1]):
        kernel_tile(jc)
    for j in peers_of(phases[0]):
        last_copy(j).wait_send()
    for j in peers_of(phases[1]):
        last_copy(j).start()
        later(last_copy(j).wait_send)
    own = aligned(s, CAP)
    returned[own, :] = kernel_out[own, :]

    build_gather()
    build_start()

    for phase in range(2):
        for j in peers_of(phases[phase]):
            last_copy(j).wait_recv()

        def add_rows(b, phase=phase):
            rows = aligned(b, tile)
            start[rows, :] += sum(
                dot(gather_mat[rows, source_rows(i)], returned[source_rows(i), :])
                for i in phases[phase]
            )

        loop(0, OWN // tile, add_rows)

    def fold(b, sums):
        rows = aligned(b, tile)
        cur = current[rows, :].astype(F32)
        return (
            sums[0] + jnp.sum(cur * start[rows, :], axis=0, keepdims=True),
            sums[1] + jnp.sum(cur * cur, axis=0, keepdims=True),
        )

    none = jnp.zeros((1, NV), F32)
    cross, square = lax.fori_loop(0, OWN // tile, fold, (none, none))

    def ratio(above, below):
        return above / jnp.where(below == 0.0, 1.0, below)

    local = ratio(cross, square)

    def fold_rest(b, acc):
        rows = aligned(b, tile)
        rest = start[rows, :] - local * current[rows, :].astype(F32)
        return acc + jnp.sum(rest * rest, axis=0, keepdims=True)

    rest_sq = lax.fori_loop(0, OWN // tile, fold_rest, none)

    def combine(read, count):
        cross = sum(read(i)[0:1] for i in range(count))
        square = sum(read(i)[1:2] for i in range(count))
        alpha = ratio(cross, square)
        rest = none
        for i in range(count):
            item = read(i)
            apart = ratio(item[0:1], item[1:2]) - alpha
            rest = rest + (item[2:3] + apart * apart * item[1:2])
        return cross, square, rest

    stats_mine[...] = jnp.concatenate([cross, square, rest_sq] + [none] * 5, axis=0)

    def stat_copy(j):
        return remote(
            stats_mine, stats_in.at[s], stat_send.at[j], stat_recv.at[j], g, peers_at[j]
        )

    def stat_ring_copy(k):
        return remote(
            stats_group,
            stats_all.at[g],
            stat_ring_send.at[k],
            stat_ring_recv.at[k],
            rings_at[k],
            s,
        )

    for j in range(1, B):
        stat_copy(j).start()
        later(stat_copy(j).wait_send)
    stats_in[s] = stats_mine[...]
    for j in range(1, B):
        stat_copy(j).wait_recv()
    stats_group[...] = jnp.concatenate(
        list(combine(lambda i: stats_in[i], B)) + [none] * 5, axis=0
    )
    for k in range(1, KR):
        stat_ring_copy(k).start()
        later(stat_ring_copy(k).wait_send)
    stats_all[g] = stats_group[...]
    for k in range(1, KR):
        stat_ring_copy(k).wait_recv()
    cross, square, rest_sq = combine(lambda i: stats_all[i], KR)

    alpha = cross / square
    beta = jnp.sqrt(rest_sq / rows_total + epsilon_mean)
    lanczos[...] = jnp.concatenate([alpha, beta] + [none] * 6, axis=0)

    drain()


def finish(start_ref, current_ref, lanczos_ref, next_ref, alpha_ref, beta_ref):
    alpha = lanczos_ref[0:1, :]
    beta = lanczos_ref[1:2, :]
    next_ref[...] = ((start_ref[...] - alpha * current_ref[...].astype(F32)) / beta).astype(BF16)
    alpha_ref[...] = alpha
    beta_ref[...] = beta


def per_device(
    planes,
    current,
    previous,
    energies,
    targets,
    layer_ids,
    conduction_pairs,
    valence_pairs,
    exchange_pairs,
    screened,
    coulomb,
    beta_prev,
):
    KR, B = lax.axis_size("kring"), lax.axis_size("band")
    OWN, NV = current.shape
    SLOT, NG = conduction_pairs.shape
    CAP = SLOT // B
    NB = B // 2
    NH = NV // 2
    GC = NG // NB
    GD = NG // B
    CH = SLOT // planes
    KY = KR // 2
    GY = NG // KY
    NQ = B
    NE = NH // NQ
    LANE = min(128, NH)
    GL = min(128, NG)
    J = NG // GL
    by_rows = jnp.transpose(screened.reshape(KR, 2, GD, 2, J, GL), (0, 1, 2, 4, 3, 5)).reshape(
        2 * KR, GD * J * 2, GL
    )
    vmem = pltpu.VMEM
    dma = pltpu.SemaphoreType.DMA
    scratch = [
        vmem((OWN, NV), BF16),
        vmem((OWN, NV), BF16),
        vmem((SLOT, NG), BF16),
        vmem((SLOT, NG), BF16),
        vmem((2, GD * J * 2, GL), BF16),
        vmem((2, KR * 2, 2, GD, NG), BF16),
        vmem((B, CAP, NV), BF16),
        vmem((SLOT, NV), BF16),
        vmem((planes, 2 * NV, CH), BF16),
        vmem((OWN, SLOT), BF16),
        vmem((1, OWN), F32),
        vmem((1, SLOT), F32),
        vmem((OWN, LANE), F32),
        vmem((SLOT, LANE), F32),
        vmem((OWN, LANE), F32),
        vmem((2, NV, NG), F32),
        vmem((2, NV, NG), F32),
        vmem((2, 2, NH, NG), F32),
        vmem((2, NB, 2, NH, GC), BF16),
        vmem((2, NB, 2, NH, GC), BF16),
        vmem((KY, 2, NH, GY), BF16),
        vmem((KY, 2, NH, GY), BF16),
        vmem((NH, 2 * GC), BF16),
        vmem((NH, KR * 2 * GC), BF16),
        vmem((2, NH, NG), F32),
        vmem((2, NH, GY), F32),
        vmem((NQ, 2, NE, GY), F32),
        vmem((2, NE, GY), F32),
        vmem((2, NH, GY), F32),
        vmem((2, GY, NH), BF16),
        vmem((2, GC, NH), BF16),
        vmem((2, NG, NV), BF16),
        vmem((2, NG, NV), BF16),
        vmem((SLOT, NV), F32),
        vmem((SLOT, NV), BF16),
        vmem((SLOT, NV), BF16),
        vmem((8, NV), F32),
        vmem((B, 8, NV), F32),
        vmem((8, NV), F32),
        vmem((KR, 8, NV), F32),
        dma((5,)),
        dma((2,)),
        dma((B,)),
        dma((B,)),
        dma((2, planes)),
        dma((2, planes)),
        dma((2, NB)),
        dma((2, NB)),
        dma,
        dma,
        dma((KR,)),
        dma((KR,)),
        dma((2, KY)),
        dma((2, KY)),
        dma((2, NQ)),
        dma((2, NQ)),
        dma((KY,)),
        dma((KY,)),
        dma((NB,)),
        dma((NB,)),
        dma((NB,)),
        dma((NB,)),
        dma((B,)),
        dma((B,)),
        dma((B,)),
        dma((B,)),
        dma((KR,)),
        dma((KR,)),
    ]
    in_vmem = pl.BlockSpec(memory_space=pltpu.VMEM)
    in_hbm = pl.BlockSpec(memory_space=pl.ANY)
    start, lanczos = pl.pallas_call(
        functools.partial(kernel, (KR, B, planes, CAP, OWN, SLOT, NG, NV)),
        out_shape=(
            jax.ShapeDtypeStruct((OWN, NV), F32),
            jax.ShapeDtypeStruct((8, NV), F32),
        ),
        in_specs=[in_vmem] * 5 + [in_hbm] * 6,
        out_specs=(in_vmem, in_vmem),
        scratch_shapes=scratch,
        compiler_params=pltpu.CompilerParams(
            collective_id=0, has_side_effects=True, vmem_limit_bytes=62 * 1024 * 1024
        ),
    )(
        targets.reshape(1, OWN),
        layer_ids.reshape(SLOT // LANE, LANE),
        energies.reshape(1, OWN),
        coulomb,
        beta_prev.reshape(1, NV),
        current,
        previous,
        conduction_pairs,
        valence_pairs,
        exchange_pairs,
        by_rows,
    )
    rows = OWN // 4
    next_vector, alpha, beta = pl.pallas_call(
        finish,
        grid=(4,),
        out_shape=(
            jax.ShapeDtypeStruct((OWN, NV), BF16),
            jax.ShapeDtypeStruct((1, NV), F32),
            jax.ShapeDtypeStruct((1, NV), F32),
        ),
        in_specs=[
            pl.BlockSpec((rows, NV), lambda b: (b, 0)),
            pl.BlockSpec((rows, NV), lambda b: (b, 0)),
            pl.BlockSpec((8, NV), lambda b: (0, 0)),
        ],
        out_specs=(
            pl.BlockSpec((rows, NV), lambda b: (b, 0)),
            pl.BlockSpec((1, NV), lambda b: (0, 0)),
            pl.BlockSpec((1, NV), lambda b: (0, 0)),
        ),
    )(start, current, lanczos)
    return next_vector, alpha.reshape(NV), beta.reshape(NV)


def solution(mesh):
    in_specs = (
        P(("kring", "band"), None),
        P(("kring", "band"), None),
        P(("kring", "band")),
        P(("kring", "band")),
        P(("kring", "band")),
        P(("kring", "band"), None),
        P(("kring", "band"), None),
        P(("kring", "band"), None),
        P(None, None, "band", None, None),
        P(),
        P(),
    )
    out_specs = (P(("kring", "band"), None), P(), P())
    planes = max(2, mesh.shape["band"] // 4)
    return jax.shard_map(
        functools.partial(per_device, planes),
        mesh=mesh,
        in_specs=in_specs,
        out_specs=out_specs,
        check_vma=False,
    )
```
